32 devices in a mesh: subset: 2 (over core), slab: 16 (over z, y, x).
Axes of the slice: x: 2, y: 2, z: 4, core: 2. Of those that a mesh axis runs over, the one named last changes fastest.
Arguments:
- z_field: float32 [1, 2048, 2048], P(None, 'slab'), may hold values from -6 to 6
- duals: float32 [2, 1, 2048, 2048], P('subset', None, 'slab'), may hold values from -3 to 3
- tiles: bfloat16 [2, 128, 128, 128], P('subset', 'slab'), may hold values from -0.1875 to 0.1875
- ray_index: int32 [2, 128], P('subset', 'slab'), may hold values from 0 to 15
- pixel_index: int32 [2, 128], P('subset', 'slab'), may hold values from 0 to 2047, as said below
- measured: float32 [2, 1, 2048], P('subset'), may hold values from -6 to 6
- step_size: float32 [2], P('subset'), may hold values from 0.2 to 0.6
- kernel: float32 [3, 3, 3], replicated, may hold values from -0.6 to 0.6
Outputs:
- new_field: float32 [1, 2048, 2048], P(None, 'slab')
- new_duals: float32 [2, 1, 2048, 2048], P('subset', None, 'slab')
The draws below stay inside these ranges and needn't reach their ends.
Inputs may be any that keep to these rules, and one draw needn't show every extreme that they name: `pixel_index`: for each subset and each slab owner, the 8 tiles of the owner name 8 different pixel blocks of its slab.
All inputs are finite; a program needn't handle non-finite values.
Results may differ from the reference program's by a relative error of at most 0.0028.
Values may be sent and summed in bfloat16 or wider, within the bound.
A program may use at most 128 MiB of HBM per device.

```python
import math
import jax
import jax.numpy as jnp
from jax import lax

W = 2048
BLOCK = 128
SL = 1
NBLK = 8
SUBSETS = 2
PIX_DEV = 262144
RAYS = 2048
TILES = 128
N_SUBSET = 2
N_SLAB = 16


def draw_pixel_index(key, part):
    block_count = PIX_DEV // BLOCK
    row_count = SUBSETS * N_SLAB
    row_keys = jax.random.split(jax.random.fold_in(key, 17), row_count)
    orders = jax.vmap(lambda single: jax.random.permutation(single, block_count))(row_keys)
    return orders[:, :NBLK].reshape(SUBSETS, N_SLAB * NBLK).astype(jnp.int32)


def set_ends(drawn, key, smallest, largest):
    extent = drawn.shape
    place = [jax.random.randint(jax.random.fold_in(key, axis), (), 0, extent[axis]) for axis in range(len(extent))]
    drawn = drawn.at[tuple(place)].set(smallest)
    longest = extent.index(max(extent))
    place[longest] = (place[longest] + 1) % extent[longest]
    return drawn.at[tuple(place)].set(largest)


def shard_levels(key, shape, pieces, smallest, largest):
    factor_of, own = 1.0, jax.random.fold_in(key, 6)
    for axis_at, blocks in pieces:
        draws = jnp.exp(jax.random.uniform(jax.random.fold_in(own, axis_at), (blocks,), jnp.float32, smallest / len(pieces), largest / len(pieces)))
        factor_of = factor_of * jnp.repeat(draws, shape[axis_at] // blocks).reshape([-1 if axis == axis_at else 1 for axis in range(len(shape))])
    return factor_of


def noise(own_key, shape, scale, reach, cuts=(), kind=jnp.bfloat16):
    loudness = shard_levels(own_key, shape, cuts, -0.22, 0.18) if cuts else 1.0
    result = jax.random.normal(own_key, shape, jnp.float32) * scale * loudness
    return jnp.minimum(jnp.maximum(result, -reach), reach).astype(kind)


def setup_inputs(seed: int = 0) -> dict:
    arg_keys = jax.random.split(jax.random.key(seed), 9)
    return {
        "z_field": noise(arg_keys[0], (SL, W, W), 1.0, 6.0, ((1, 16),), jnp.float32),
        "duals": noise(arg_keys[1], (SUBSETS, SL, W, W), 0.5, 3.0, ((0, 2), (2, 16)), jnp.float32),
        "tiles": noise(arg_keys[2], (SUBSETS, TILES, BLOCK, BLOCK), (N_SLAB * NBLK * BLOCK * BLOCK // RAYS) ** -0.5, 0.1875, ((0, 2), (1, 16))),
        "ray_index": set_ends(jax.random.randint(arg_keys[3], (SUBSETS, TILES), 0, RAYS // BLOCK), jax.random.fold_in(arg_keys[3], 1), 0, (RAYS // BLOCK) - 1).astype(jnp.int32),
        "pixel_index": draw_pixel_index(jax.random.fold_in(arg_keys[8], 71), 0),
        "measured": noise(arg_keys[5], (SUBSETS, SL, RAYS), 1.0, 6.0, ((0, 2),), jnp.float32),
        "step_size": jnp.clip(jnp.exp(math.log(0.6) - 1.0986123 * jax.random.uniform(arg_keys[6], (SUBSETS,), jnp.float32) ** shard_levels(arg_keys[6], (SUBSETS,), ((0, 2),), -0.2, 0.2)), 0.2, 0.6),
        "kernel": noise(arg_keys[7], (3, 3, 3), 0.15, 0.6, (), jnp.float32),
    }


def one_subset(z_field, dual_part, tile_part, ray_part, pixel_part, measured_part, step_value):
    start_field = z_field - dual_part
    flat_blocks = start_field.astype(jnp.bfloat16).reshape(SL, W * W // BLOCK, BLOCK)
    owner_index = jnp.arange(N_SLAB * NBLK, dtype=jnp.int32) // NBLK
    global_pixel = (owner_index * (PIX_DEV // BLOCK) + pixel_part).astype(jnp.int32)
    tile_values = tile_part.astype(jnp.float32)
    chosen_blocks = jnp.take(flat_blocks, global_pixel, axis=1).astype(jnp.float32)
    contrib = jnp.einsum('snp,nrp->nsr', chosen_blocks, tile_values, precision=lax.Precision.HIGHEST)
    projected = jax.ops.segment_sum(contrib, ray_part, num_segments=RAYS // BLOCK)
    projected = jnp.transpose(projected, (1, 0, 2)).reshape(SL, RAYS)
    residual = (projected - measured_part).astype(jnp.bfloat16)
    picked_rays = jnp.take(residual.reshape(SL, RAYS // BLOCK, BLOCK), ray_part, axis=1).astype(jnp.float32)
    back_terms = jnp.einsum('snr,nrp->nsp', picked_rays, tile_values, precision=lax.Precision.HIGHEST)
    back_sum = jax.ops.segment_sum(back_terms, global_pixel, num_segments=W * W // BLOCK)
    back_sum = jnp.transpose(back_sum, (1, 0, 2)).reshape(SL, W, W)
    return start_field - step_value * (W / math.sqrt(RAYS)) * back_sum

def reference(z_field, duals, tiles, ray_index, pixel_index, measured, step_size, kernel):

    def apply_subset(packed):
        return one_subset(z_field, packed[0], packed[1], packed[2], packed[3], packed[4], packed[5])
    estimates = lax.map(apply_subset, (duals, tiles, ray_index, pixel_index, measured, step_size))
    average = lax.optimization_barrier(jnp.sum(estimates + duals, axis=0)) / N_SUBSET
    padded = jnp.pad(average, 1)
    filtered = jnp.zeros_like(average)
    for offset_a in range(3):
        for offset_b in range(3):
            for offset_c in range(3):
                filtered = filtered + kernel[offset_a, offset_b, offset_c] * padded[offset_a:offset_a + SL, offset_b:offset_b + W, offset_c:offset_c + W]
    new_field = average + filtered
    new_duals = duals + estimates - new_field[None]
    return (new_field, new_duals)
```

```python
import functools
import math

import jax
import jax.numpy as jnp
from jax import lax
from jax.experimental import pallas as pl
from jax.experimental.pallas import tpu as pltpu
from jax.sharding import PartitionSpec as P

MESH = pl.DeviceIdType.MESH


def split_group(count):
    inner = 1
    while inner * inner * 4 <= count and count % (inner * 2) == 0:
        inner *= 2
    return inner, count // inner


def gather_kernel(z_hbm, dual_hbm, pix_ref, start_ref, z_v, dual_v, z_sem, dual_sem):
    slices, nblk, block = start_ref.shape
    col_blocks = z_hbm.shape[2] // block
    copies = []
    for n in range(nblk):
        pixel = pix_ref[0, n]
        row = pl.multiple_of(lax.div(pixel, col_blocks * 8) * 8, 8)
        col = pl.multiple_of(lax.rem(pixel, col_blocks) * block, block)
        at = (slice(None), pl.ds(row, 8), pl.ds(col, block))
        copies.append(pltpu.make_async_copy(z_hbm.at[at], z_v.at[n], z_sem.at[n]))
        copies.append(pltpu.make_async_copy(dual_hbm.at[(0, *at)], dual_v.at[n], dual_sem.at[n]))
    for copy in copies:
        copy.start()
    for copy in copies:
        copy.wait()
    sublanes = lax.broadcasted_iota(jnp.int32, (8, block), 0)
    tile_rows = lax.broadcasted_iota(jnp.int32, (nblk, block), 0)
    for s in range(slices):
        start = jnp.zeros((nblk, block), jnp.float32)
        for n in range(nblk):
            row = lax.rem(lax.div(pix_ref[0, n], col_blocks), 8)
            part = jnp.where(sublanes == row, z_v[n, s] - dual_v[n, s], 0.0)
            start = jnp.where(tile_rows == n, jnp.sum(part, axis=0, keepdims=True), start)
        start_ref[s] = start


def rays_kernel(
    sub_n, slab_n,
    z_hbm, start_ref, tile_hbm, meas_ref, ray_ref, pix_ref, step_ref,
    delta_out, pix_out, halo_out,
    tile_v, pix_v, got_in, got_out, delta_v, pixels_v, halo_v,
    load_sem, in_send, in_recv, out_send, out_recv,
    pix_send, pix_recv, halo_send, halo_recv, fin_send, fin_recv,
):
    slices, rows, width = z_hbm.shape
    nblk, block = tile_v.shape[0], tile_v.shape[1]
    ray_blocks = got_in.shape[2]
    col_blocks = width // block
    inner, outer = split_group(slab_n)
    sub = lax.axis_index("subset")
    slab = lax.axis_index("slab")
    lane = slab % inner
    tier = slab // inner
    has_up = slab > 0
    has_down = slab < slab_n - 1

    load = pltpu.make_async_copy(tile_hbm.at[0], tile_v, load_sem)
    load.start()

    pixels_v[...] = jnp.zeros_like(pixels_v)
    delta_v[...] = jnp.zeros_like(delta_v)
    halo_v[...] = jnp.zeros_like(halo_v)

    in_peers = [(sub, tier * inner + (lane + k) % inner) for k in range(1, inner)]
    out_peers = [(sub, ((tier + k) % outer) * inner + lane) for k in range(1, outer)]
    sub_peers = [((sub + k) % sub_n, slab) for k in range(1, sub_n)]
    barrier = pltpu.get_barrier_semaphore()
    for peer in in_peers + out_peers + sub_peers:
        pl.semaphore_signal(barrier, inc=1, device_id=peer, device_id_type=MESH)

    @pl.when(has_up)
    def _():
        for k in range(sub_n):
            pl.semaphore_signal(
                barrier, inc=1, device_id=((sub + k) % sub_n, slab - 1), device_id_type=MESH
            )

    @pl.when(has_down)
    def _():
        for k in range(sub_n):
            pl.semaphore_signal(
                barrier, inc=1, device_id=((sub + k) % sub_n, slab + 1), device_id_type=MESH
            )

    lanes = lax.broadcasted_iota(jnp.int32, (8, block), 1)
    mine = jnp.zeros((8, block), jnp.int32)
    for n in range(nblk):
        mine = jnp.where(lanes == n, pix_ref[0, n], mine)
    pix_v[...] = mine
    pixels_v[0, sub] = mine

    ray_rows = lax.broadcasted_iota(jnp.int32, (ray_blocks, block), 0)
    hot_rows = lax.broadcasted_iota(jnp.int32, (nblk, ray_blocks), 0)
    hot_cols = lax.broadcasted_iota(jnp.int32, (nblk, ray_blocks), 1)
    hot = jnp.zeros((nblk, ray_blocks), jnp.float32)
    for n in range(nblk):
        here = jnp.where(hot_cols == ray_ref[0, n], 1.0, 0.0)
        hot = jnp.where(hot_rows == n, here, hot)
    hot = hot.astype(jnp.bfloat16)
    load.wait()
    for s in range(slices):
        start = start_ref[s].astype(jnp.bfloat16)
        total = jnp.zeros((ray_blocks, block), jnp.float32)
        for n in range(nblk):
            term = lax.dot_general(
                start, tile_v[n], (((1,), (1,)), ((), ())), preferred_element_type=jnp.float32
            )
            total = total + jnp.where(ray_rows == ray_ref[0, n], term[n : n + 1], 0.0)
        got_in[lane, s] = total

    pl.semaphore_wait(
        barrier,
        len(in_peers + out_peers + sub_peers)
        + sub_n * (has_up.astype(jnp.int32) + has_down.astype(jnp.int32)),
    )

    def spread(src, dst, peers, send, recv):
        return [
            pltpu.make_async_remote_copy(
                src_ref=src, dst_ref=dst, send_sem=send.at[k], recv_sem=recv.at[k],
                device_id=peer, device_id_type=MESH,
            )
            for k, peer in enumerate(peers)
        ]

    ins = spread(got_in.at[lane], got_in.at[lane], in_peers, in_send, in_recv)
    for copy in ins:
        copy.start()

    pix_subs = spread(pix_v, pixels_v.at[0, sub], sub_peers, pix_send.at[0], pix_recv.at[0])
    above = [((sub + k) % sub_n, slab - 1) for k in range(sub_n)]
    below = [((sub + k) % sub_n, slab + 1) for k in range(sub_n)]
    pix_up = spread(pix_v, pixels_v.at[2, sub], above, pix_send.at[1], pix_recv.at[1])
    pix_down = spread(pix_v, pixels_v.at[1, sub], below, pix_send.at[2], pix_recv.at[2])
    halo_up = spread(
        z_hbm.at[:, pl.ds(0, 1)], halo_v.at[1], above[:1], halo_send.at[0], halo_recv.at[0]
    )
    halo_down = spread(
        z_hbm.at[:, pl.ds(rows - 1, 1)], halo_v.at[0], below[:1], halo_send.at[1], halo_recv.at[1]
    )
    for copy in pix_subs:
        copy.start()

    @pl.when(has_up)
    def _():
        for copy in pix_up + halo_up:
            copy.start()

    @pl.when(has_down)
    def _():
        for copy in pix_down + halo_down:
            copy.start()

    for copy in ins:
        copy.wait_recv()
    group = got_in[0]
    for k in range(1, inner):
        group = group + got_in[k]
    got_out[tier] = group
    outs = spread(got_out.at[tier], got_out.at[tier], out_peers, out_send, out_recv)
    for copy in outs:
        copy.start()
    targets = []
    for s in range(slices):
        target = jnp.zeros((ray_blocks, block), jnp.float32)
        for k in range(ray_blocks):
            piece = meas_ref[0, pl.ds(s, 1), pl.ds(k * block, block)]
            target = jnp.where(ray_rows == k, piece, target)
        targets.append(target)
    for copy in outs:
        copy.wait_recv()
    full = got_out[0]
    for k in range(1, outer):
        full = full + got_out[k]
    scale = step_ref[0] * (width / math.sqrt(ray_blocks * block))
    tile_rows = lax.broadcasted_iota(jnp.int32, (nblk, block), 0)
    for s in range(slices):
        residual = (full[s] - targets[s]).astype(jnp.bfloat16)
        picked = jnp.dot(hot, residual, preferred_element_type=jnp.float32).astype(jnp.bfloat16)
        delta = jnp.zeros((nblk, block), jnp.float32)
        for n in range(nblk):
            term = jnp.dot(picked, tile_v[n], preferred_element_type=jnp.float32)
            delta = jnp.where(tile_rows == n, term, delta)
        delta = delta * scale
        delta_v[0, sub, s] = delta

    own = delta_v.at[0, sub]
    fin_subs = spread(own, delta_v.at[0, sub], sub_peers, fin_send.at[0], fin_recv.at[0])
    fin_up = spread(own, delta_v.at[2, sub], above, fin_send.at[1], fin_recv.at[1])
    fin_down = spread(own, delta_v.at[1, sub], below, fin_send.at[2], fin_recv.at[2])

    @pl.when(has_up)
    def _():
        for copy in fin_up:
            copy.start()

    @pl.when(has_down)
    def _():
        for copy in fin_down:
            copy.start()

    for copy in fin_subs:
        copy.start()
    for copy in ins + outs:
        copy.wait_send()
    for copy in pix_subs + fin_subs:
        copy.wait()

    @pl.when(has_up)
    def _():
        for copy in pix_up + halo_up + fin_up:
            copy.wait_send()
        for copy in pix_down + halo_down + fin_down:
            copy.wait_recv()

    @pl.when(has_down)
    def _():
        for copy in pix_down + halo_down + fin_down:
            copy.wait_send()
        for copy in pix_up + halo_up + fin_up:
            copy.wait_recv()

    delta_out[...] = delta_v[...]
    pix_out[...] = pixels_v[...]
    halo_out[...] = halo_v[...]


def field_kernel(
    z_hbm, delta_ref, pix_ref, halo_ref, w_ref,
    field_hbm, dual_hbm,
    avg_v, own_v, field_v, dual_v, load_sem, store_sem,
):
    slices, rows, width = own_v.shape
    sub_n, nblk, block = delta_ref.shape[1], delta_ref.shape[3], delta_ref.shape[4]
    col_blocks = width // block
    sub = lax.axis_index("subset")
    loads = [
        pltpu.make_async_copy(z_hbm, avg_v.at[:, pl.ds(8, rows)], load_sem.at[0]),
        pltpu.make_async_copy(z_hbm, own_v, load_sem.at[1]),
    ]
    for load in loads:
        load.start()
    avg_v[:, pl.ds(7, 1), :] = halo_ref[0]
    avg_v[:, pl.ds(8 + rows, 1), :] = halo_ref[1]
    for load in loads:
        load.wait()
    share = 1.0 / sub_n
    sublanes = lax.broadcasted_iota(jnp.int32, (8, block), 0)
    for place in range(3):
        for i in range(sub_n):
            for n in range(nblk):
                pixel = pix_ref[place, i, 0, n]
                row = pixel // col_blocks
                col = pl.multiple_of((pixel % col_blocks) * block, block)
                if place == 0:
                    row = row + 8
                elif place == 1:
                    row = jnp.where(row == rows - 1, 7, 0)
                else:
                    row = jnp.where(row == 0, 8 + rows, 0)
                base = pl.multiple_of(row // 8 * 8, 8)
                for s in range(slices):
                    at = (s, pl.ds(base, 8), pl.ds(col, block))
                    value = delta_ref[place, i, s, pl.ds(n, 1), :] * share
                    avg_v[at] = avg_v[at] - jnp.where(sublanes == row % 8, value, 0.0)
    for n in range(nblk):
        pixel = pix_ref[0, sub, 0, n]
        row = pixel // col_blocks
        col = pl.multiple_of((pixel % col_blocks) * block, block)
        base = pl.multiple_of(row // 8 * 8, 8)
        for s in range(slices):
            at = (s, pl.ds(base, 8), pl.ds(col, block))
            value = delta_ref[0, sub, s, pl.ds(n, 1), :]
            own_v[at] = own_v[at] - jnp.where(sublanes == row % 8, value, 0.0)

    columns = lax.broadcasted_iota(jnp.int32, (8, width), 1)
    weights = [[[w_ref[a, b, c] for c in range(3)] for b in range(3)] for a in range(3)]

    def copies(s, g):
        at = pl.ds(pl.multiple_of(g * 8, 8), 8)
        return (
            pltpu.make_async_copy(field_v.at[s, at], field_hbm.at[s, at], store_sem.at[0]),
            pltpu.make_async_copy(dual_v.at[s, at], dual_hbm.at[0, s, at], store_sem.at[1]),
        )

    for s in range(slices):
        def step(g, carry, s=s):
            base = pl.multiple_of(g * 8, 8)
            at = pl.ds(base, 8)
            sums = [None, None, None]
            for a in range(3):
                if not 0 <= s + a - 1 < slices:
                    continue
                window = avg_v[s + a - 1, pl.ds(base, 24), :]
                for b in range(3):
                    moved = window[7 + b : 15 + b]
                    if a == 1 and b == 1:
                        middle = moved
                    for c in range(3):
                        term = weights[a][b][c] * moved
                        sums[c] = term if sums[c] is None else sums[c] + term
            left = jnp.where(columns == 0, 0.0, pltpu.roll(sums[0], 1, 1))
            right = jnp.where(columns == width - 1, 0.0, pltpu.roll(sums[2], width - 1, 1))
            field = middle + (sums[1] + left + right)
            field_v[s, at] = field
            dual_v[s, at] = own_v[s, at] - field
            for copy in copies(s, g):
                copy.start()
            return carry

        lax.fori_loop(0, rows // 8, step, 0)
    pltpu.make_async_copy(field_v, field_hbm, store_sem.at[0]).wait()
    pltpu.make_async_copy(dual_v, dual_hbm.at[0], store_sem.at[1]).wait()


def body(sub_n, slab_n, z_field, duals, tiles, ray_index, pixel_index, measured, step_size, kernel):
    slices, rows, width = z_field.shape
    nblk, block = tiles.shape[1], tiles.shape[2]
    ray_blocks = measured.shape[2] // block
    inner, outer = split_group(slab_n)
    hbm = pl.BlockSpec(memory_space=pl.ANY)
    vmem = pl.BlockSpec(memory_space=pltpu.VMEM)
    smem = pl.BlockSpec(memory_space=pltpu.SMEM)
    dma = pltpu.SemaphoreType.DMA
    delta_shape = (3, sub_n, slices, nblk, block)
    pix_shape = (3, sub_n, 8, block)
    halo_shape = (2, slices, 1, width)
    start = pl.pallas_call(
        gather_kernel,
        out_shape=jax.ShapeDtypeStruct((slices, nblk, block), jnp.float32),
        in_specs=[hbm, hbm, smem],
        out_specs=vmem,
        scratch_shapes=[
            pltpu.VMEM((nblk, slices, 8, block), jnp.float32),
            pltpu.VMEM((nblk, slices, 8, block), jnp.float32),
            dma((nblk,)), dma((nblk,)),
        ],
        name="gather",
    )(z_field, duals, pixel_index)
    delta, pixels, halo = pl.pallas_call(
        functools.partial(rays_kernel, sub_n, slab_n),
        out_shape=(
            jax.ShapeDtypeStruct(delta_shape, jnp.float32),
            jax.ShapeDtypeStruct(pix_shape, jnp.int32),
            jax.ShapeDtypeStruct(halo_shape, jnp.float32),
        ),
        in_specs=[hbm, vmem, hbm, vmem, smem, smem, smem],
        out_specs=(vmem, vmem, vmem),
        scratch_shapes=[
            pltpu.VMEM((nblk, block, block), jnp.bfloat16),
            pltpu.VMEM((8, block), jnp.int32),
            pltpu.VMEM((inner, slices, ray_blocks, block), jnp.float32),
            pltpu.VMEM((outer, slices, ray_blocks, block), jnp.float32),
            pltpu.VMEM(delta_shape, jnp.float32),
            pltpu.VMEM(pix_shape, jnp.int32),
            pltpu.VMEM(halo_shape, jnp.float32),
            dma,
            dma((inner,)), dma((inner,)),
            dma((outer,)), dma((outer,)),
            dma((3, sub_n)), dma((3, sub_n)),
            dma((2, 1)), dma((2, 1)),
            dma((3, sub_n)), dma((3, sub_n)),
        ],
        compiler_params=pltpu.CompilerParams(collective_id=0, has_side_effects=True),
        name="rays",
    )(z_field, start, tiles, measured, ray_index, pixel_index, step_size)
    return pl.pallas_call(
        field_kernel,
        out_shape=(
            jax.ShapeDtypeStruct((slices, rows, width), jnp.float32),
            jax.ShapeDtypeStruct((1, slices, rows, width), jnp.float32),
        ),
        in_specs=[hbm, vmem, smem, vmem, smem],
        out_specs=(hbm, hbm),
        scratch_shapes=[
            pltpu.VMEM((slices, rows + 16, width), jnp.float32),
            pltpu.VMEM((slices, rows, width), jnp.float32),
            pltpu.VMEM((slices, rows, width), jnp.float32),
            pltpu.VMEM((slices, rows, width), jnp.float32),
            dma((2,)), dma((2,)),
        ],
        name="field",
    )(z_field, delta, pixels, halo, kernel)


def solution(mesh):
    placed = (
        P(None, "slab", None),
        P("subset", None, "slab", None),
        P("subset", "slab", None, None),
        P("subset", "slab"),
        P("subset", "slab"),
        P("subset", None, None),
        P("subset"),
        P(),
    )
    return jax.shard_map(
        functools.partial(body, mesh.shape["subset"], mesh.shape["slab"]),
        mesh=mesh,
        in_specs=placed,
        out_specs=(P(None, "slab", None), P("subset", None, "slab", None)),
        check_vma=False,
    )
```

```python
import functools
import math

import jax
import jax.numpy as jnp
from jax import lax
from jax.experimental import pallas as pl
from jax.experimental.pallas import tpu as pltpu
from jax.sharding import PartitionSpec as P

MESH = pl.DeviceIdType.MESH


def split_group(count):
    inner = 1
    while inner < min(count, 16) and count % (inner * 2) == 0:
        inner *= 2
    return inner, count // inner


def rays_kernel(
    sub_n, slab_n,
    z_hbm, dual_hbm, tile_hbm, meas_hbm, ray_hbm, pix_hbm, step_hbm, w_hbm,
    delta_out, pix_out, base_out,
    meas_ref, ray_ref, pix_ref, step_ref, w_ref, z_v, dual_v, base_v, tile_v, pix_v, got_in, got_out, delta_v, pixels_v, halo_v,
    load_sem, base_sem, in_send, in_recv, out_send, out_recv,
    pix_send, pix_recv, halo_send, halo_recv, fin_send, fin_recv,
):
    slices, rows, width = z_hbm.shape
    nblk, block = tile_v.shape[0], tile_v.shape[1]
    ray_blocks = got_in.shape[2]
    col_blocks = width // block
    inner, outer = split_group(slab_n)
    sub = lax.axis_index("subset")
    slab = lax.axis_index("slab")
    lane = slab % inner
    tier = slab // inner
    has_up = slab > 0
    has_down = slab < slab_n - 1

    loads = [
        pltpu.make_async_copy(z_hbm, z_v.at[:, pl.ds(8, rows)], load_sem.at[0]),
        pltpu.make_async_copy(dual_hbm.at[0], dual_v, load_sem.at[1]),
        pltpu.make_async_copy(tile_hbm.at[0], tile_v, load_sem.at[2]),
    ]
    pairs = [
        (meas_hbm, meas_ref), (ray_hbm, ray_ref), (pix_hbm, pix_ref),
        (step_hbm, step_ref), (w_hbm, w_ref),
    ]
    smalls = [
        pltpu.make_async_copy(src, dst, load_sem.at[3 + i]) for i, (src, dst) in enumerate(pairs)
    ]
    for load in smalls + loads:
        load.start()

    pixels_v[...] = jnp.zeros_like(pixels_v)
    delta_v[...] = jnp.zeros_like(delta_v)
    halo_v[...] = jnp.zeros_like(halo_v)

    in_peers = [(sub, tier * inner + (lane + k) % inner) for k in range(1, inner)]
    out_peers = [(sub, ((tier + k) % outer) * inner + lane) for k in range(1, outer)]
    sub_peers = [((sub + k) % sub_n, slab) for k in range(1, sub_n)]
    barrier = pltpu.get_barrier_semaphore()
    for peer in in_peers + out_peers + sub_peers:
        pl.semaphore_signal(barrier, inc=1, device_id=peer, device_id_type=MESH)

    @pl.when(has_up)
    def _():
        for k in range(sub_n):
            pl.semaphore_signal(
                barrier, inc=1, device_id=((sub + k) % sub_n, slab - 1), device_id_type=MESH
            )

    @pl.when(has_down)
    def _():
        for k in range(sub_n):
            pl.semaphore_signal(
                barrier, inc=1, device_id=((sub + k) % sub_n, slab + 1), device_id_type=MESH
            )

    for load in smalls:
        load.wait()
    columns = lax.broadcasted_iota(jnp.int32, (8, width), 1)
    weights = [[[w_ref[a, b, c] for c in range(3)] for b in range(3)] for a in range(3)]

    def stencil(low, high):
        for s in range(slices):
            def step(g, carry, s=s):
                base = pl.multiple_of(g * 8, 8)
                sums = [None, None, None]
                for a in range(3):
                    if not 0 <= s + a - 1 < slices:
                        continue
                    window = z_v[s + a - 1, pl.ds(base, 24), :]
                    for b in range(3):
                        moved = window[7 + b : 15 + b]
                        if a == 1 and b == 1:
                            middle = moved
                        for c in range(3):
                            term = weights[a][b][c] * moved
                            sums[c] = term if sums[c] is None else sums[c] + term
                left = jnp.where(columns == 0, 0.0, pltpu.roll(sums[0], 1, 1))
                right = jnp.where(columns == width - 1, 0.0, pltpu.roll(sums[2], width - 1, 1))
                base_v[s, pl.ds(base, 8), :] = middle + (sums[1] + left + right)
                return carry

            lax.fori_loop(low, high, step, 0)

    groups = rows // 8
    first_cut = 1 + max(groups - 2, 0) * 5 // 14
    second_cut = 1 + max(groups - 2, 0) * 10 // 14

    lanes = lax.broadcasted_iota(jnp.int32, (8, block), 1)
    mine = jnp.zeros((8, block), jnp.int32)
    for n in range(nblk):
        mine = jnp.where(lanes == n, pix_ref[0, n], mine)
    pix_v[...] = mine
    pixels_v[0, sub] = mine

    ray_rows = lax.broadcasted_iota(jnp.int32, (ray_blocks, block), 0)
    hot_rows = lax.broadcasted_iota(jnp.int32, (nblk, ray_blocks), 0)
    hot_cols = lax.broadcasted_iota(jnp.int32, (nblk, ray_blocks), 1)
    hot = jnp.zeros((nblk, ray_blocks), jnp.float32)
    for n in range(nblk):
        here = jnp.where(hot_cols == ray_ref[0, n], 1.0, 0.0)
        hot = jnp.where(hot_rows == n, here, hot)
    hot = hot.astype(jnp.bfloat16)
    row_cols = lax.broadcasted_iota(jnp.int32, (nblk, rows), 1)
    row_rows = lax.broadcasted_iota(jnp.int32, (nblk, rows), 0)
    tile_rows = lax.broadcasted_iota(jnp.int32, (nblk, block), 0)
    row_hot = jnp.zeros((nblk, rows), jnp.float32)
    col_of = jnp.zeros((nblk, block), jnp.int32)
    for n in range(nblk):
        here = jnp.where(row_cols == lax.div(pix_ref[0, n], col_blocks), 1.0, 0.0)
        row_hot = jnp.where(row_rows == n, here, row_hot)
        col_of = jnp.where(tile_rows == n, lax.rem(pix_ref[0, n], col_blocks), col_of)
    row_hot = row_hot.astype(jnp.bfloat16)
    for load in loads:
        load.wait()
    for s in range(slices):
        start = jnp.zeros((nblk, block), jnp.float32)
        for c in range(col_blocks):
            at = pl.ds(c * block, block)
            part = (z_v[s, pl.ds(8, rows), at] - dual_v[s, :, at]).astype(jnp.bfloat16)
            part = jnp.dot(row_hot, part, preferred_element_type=jnp.float32)
            start = jnp.where(col_of == c, part, start)
        start = start.astype(jnp.bfloat16)
        total = jnp.zeros((ray_blocks, block), jnp.float32)
        for n in range(nblk):
            term = lax.dot_general(
                start, tile_v[n], (((1,), (1,)), ((), ())), preferred_element_type=jnp.float32
            )
            total = total + jnp.where(ray_rows == ray_ref[0, n], term[n : n + 1], 0.0)
        got_in[lane, s] = total

    pl.semaphore_wait(
        barrier,
        len(in_peers + out_peers + sub_peers)
        + sub_n * (has_up.astype(jnp.int32) + has_down.astype(jnp.int32)),
    )

    def spread(src, dst, peers, send, recv):
        return [
            pltpu.make_async_remote_copy(
                src_ref=src, dst_ref=dst, send_sem=send.at[k], recv_sem=recv.at[k],
                device_id=peer, device_id_type=MESH,
            )
            for k, peer in enumerate(peers)
        ]

    ins = spread(got_in.at[lane], got_in.at[lane], in_peers, in_send, in_recv)
    for copy in ins:
        copy.start()

    pix_subs = spread(pix_v, pixels_v.at[0, sub], sub_peers, pix_send.at[0], pix_recv.at[0])
    above = [((sub + k) % sub_n, slab - 1) for k in range(sub_n)]
    below = [((sub + k) % sub_n, slab + 1) for k in range(sub_n)]
    pix_up = spread(pix_v, pixels_v.at[2, sub], above, pix_send.at[1], pix_recv.at[1])
    pix_down = spread(pix_v, pixels_v.at[1, sub], below, pix_send.at[2], pix_recv.at[2])
    halo_up = spread(
        z_hbm.at[:, pl.ds(0, 1)], halo_v.at[1], above[:1], halo_send.at[0], halo_recv.at[0]
    )
    halo_down = spread(
        z_hbm.at[:, pl.ds(rows - 1, 1)], halo_v.at[0], below[:1], halo_send.at[1], halo_recv.at[1]
    )
    for copy in pix_subs:
        copy.start()

    @pl.when(has_up)
    def _():
        for copy in pix_up + halo_up:
            copy.start()

    @pl.when(has_down)
    def _():
        for copy in pix_down + halo_down:
            copy.start()

    stencil(1, first_cut)
    for copy in ins:
        copy.wait_recv()
    group = got_in[0]
    for k in range(1, inner):
        group = group + got_in[k]
    got_out[tier] = group
    outs = spread(got_out.at[tier], got_out.at[tier], out_peers, out_send, out_recv)
    for copy in outs:
        copy.start()
    targets = []
    for s in range(slices):
        target = jnp.zeros((ray_blocks, block), jnp.float32)
        for k in range(ray_blocks):
            piece = meas_ref[0, pl.ds(s, 1), pl.ds(k * block, block)]
            target = jnp.where(ray_rows == k, piece, target)
        targets.append(target)
    stencil(first_cut, second_cut)
    for copy in outs:
        copy.wait_recv()
    full = got_out[0]
    for k in range(1, outer):
        full = full + got_out[k]
    scale = step_ref[0] * (width / math.sqrt(ray_blocks * block))
    for s in range(slices):
        residual = (full[s] - targets[s]).astype(jnp.bfloat16)
        picked = jnp.dot(hot, residual, preferred_element_type=jnp.float32).astype(jnp.bfloat16)
        delta = jnp.zeros((nblk, block), jnp.float32)
        for n in range(nblk):
            term = jnp.dot(picked, tile_v[n], preferred_element_type=jnp.float32)
            delta = jnp.where(tile_rows == n, term, delta)
        delta = delta * scale
        delta_v[0, sub, s] = delta

    own = delta_v.at[0, sub]
    fin_subs = spread(own, delta_v.at[0, sub], sub_peers, fin_send.at[0], fin_recv.at[0])
    fin_up = spread(own, delta_v.at[2, sub], above, fin_send.at[1], fin_recv.at[1])
    fin_down = spread(own, delta_v.at[1, sub], below, fin_send.at[2], fin_recv.at[2])

    @pl.when(has_up)
    def _():
        for copy in fin_up:
            copy.start()

    @pl.when(has_down)
    def _():
        for copy in fin_down:
            copy.start()

    for copy in fin_subs:
        copy.start()
    stencil(second_cut, max(groups - 1, 1))

    @pl.when(has_down)
    def _():
        for copy in halo_up:
            copy.wait_recv()

    @pl.when(has_up)
    def _():
        for copy in halo_down:
            copy.wait_recv()

    z_v[:, pl.ds(7, 1), :] = halo_v[0]
    z_v[:, pl.ds(8 + rows, 1), :] = halo_v[1]
    stencil(0, 1)
    if groups > 1:
        stencil(groups - 1, groups)
    base_copy = pltpu.make_async_copy(base_v, base_out, base_sem)
    base_copy.start()
    for copy in ins + outs:
        copy.wait_send()
    for copy in pix_subs + fin_subs:
        copy.wait()

    @pl.when(has_up)
    def _():
        for copy in pix_up + halo_up + fin_up:
            copy.wait_send()
        for copy in pix_down + fin_down:
            copy.wait_recv()

    @pl.when(has_down)
    def _():
        for copy in pix_down + halo_down + fin_down:
            copy.wait_send()
        for copy in pix_up + fin_up:
            copy.wait_recv()

    delta_out[...] = delta_v[...]
    pix_out[...] = pixels_v[...]
    base_copy.wait()


def field_kernel(
    z_hbm, base_hbm, delta_ref, pix_ref, w_ref,
    field_hbm, dual_hbm,
    field_v, own_v, load_sem, store_sem,
):
    slices, rows, width = own_v.shape
    sub_n, nblk, block = delta_ref.shape[1], delta_ref.shape[3], delta_ref.shape[4]
    col_blocks = width // block
    sub = lax.axis_index("subset")
    inside = (slice(None), pl.ds(8, rows), pl.ds(block, width))
    loads = [
        pltpu.make_async_copy(base_hbm, field_v.at[inside], load_sem.at[0]),
        pltpu.make_async_copy(z_hbm, own_v, load_sem.at[1]),
    ]
    for load in loads:
        load.start()
    weights = [[[w_ref[a, b, c] for c in range(3)] for b in range(3)] for a in range(3)]
    share = -1.0 / sub_n
    sublanes = lax.broadcasted_iota(jnp.int32, (8, block), 0)
    window_rows = lax.broadcasted_iota(jnp.int32, (16, 3 * block), 0)
    zeros = jnp.zeros((1, block), jnp.float32)

    def patch(place, i, n, row, col):
        base = pl.multiple_of((row - 1) // 8 * 8, 8)
        step = window_rows - (row - 1 - base)
        for s in range(slices):
            delta = delta_ref[place, i, s, pl.ds(n, 1), :] * share
            wide = jnp.concatenate([zeros, delta, zeros], axis=1)
            left = pltpu.roll(wide, 1, 1)
            right = pltpu.roll(wide, 3 * block - 1, 1)
            for a in range(3):
                out = s + 1 - a
                if not 0 <= out < slices:
                    continue
                sums = [w[0] * left + w[1] * wide + w[2] * right for w in weights[a]]
                if a == 1:
                    sums[1] = sums[1] + wide
                add = jnp.where(step == 2, sums[0], 0.0)
                add = jnp.where(step == 1, sums[1], add)
                add = jnp.where(step == 0, sums[2], add)
                at = (out, pl.ds(base, 16), pl.ds(col, 3 * block))
                field_v[at] = field_v[at] + add

    for load in loads:
        load.wait()
    for place in range(3):
        for i in range(sub_n):
            for n in range(nblk):
                pixel = pix_ref[place, i, 0, n]
                row = pixel // col_blocks
                col = pl.multiple_of((pixel % col_blocks) * block, block)
                if place == 0:
                    patch(place, i, n, row + 8, col)
                elif place == 1:
                    pl.when(row == rows - 1)(functools.partial(patch, place, i, n, 7, col))
                else:
                    pl.when(row == 0)(functools.partial(patch, place, i, n, rows + 8, col))
    stores = [pltpu.make_async_copy(field_v.at[inside], field_hbm, store_sem.at[0])]
    stores[0].start()
    for n in range(nblk):
        pixel = pix_ref[0, sub, 0, n]
        row = pixel // col_blocks
        col = pl.multiple_of((pixel % col_blocks) * block, block)
        base = pl.multiple_of(row // 8 * 8, 8)
        for s in range(slices):
            at = (s, pl.ds(base, 8), pl.ds(col, block))
            value = delta_ref[0, sub, s, pl.ds(n, 1), :]
            own_v[at] = own_v[at] - jnp.where(sublanes == row % 8, value, 0.0)
    parts = 4 if rows % 32 == 0 else 1
    size = rows // parts
    for part in range(parts):
        for s in range(slices):
            def step(g, carry, s=s, part=part):
                at = pl.multiple_of(part * size + g * 8, 8)
                field = field_v[s, pl.ds(at + 8, 8), pl.ds(block, width)]
                own_v[s, pl.ds(at, 8), :] = own_v[s, pl.ds(at, 8), :] - field
                return carry

            lax.fori_loop(0, size // 8, step, 0)
        span = (slice(None), pl.ds(part * size, size))
        stores.append(
            pltpu.make_async_copy(own_v.at[span], dual_hbm.at[(0, *span)], store_sem.at[1 + part])
        )
        stores[-1].start()
    for store in stores:
        store.wait()


def body(sub_n, slab_n, z_field, duals, tiles, ray_index, pixel_index, measured, step_size, kernel):
    slices, rows, width = z_field.shape
    nblk, block = tiles.shape[1], tiles.shape[2]
    ray_blocks = measured.shape[2] // block
    inner, outer = split_group(slab_n)
    hbm = pl.BlockSpec(memory_space=pl.ANY)
    vmem = pl.BlockSpec(memory_space=pltpu.VMEM)
    smem = pl.BlockSpec(memory_space=pltpu.SMEM)
    dma = pltpu.SemaphoreType.DMA
    delta_shape = (3, sub_n, slices, nblk, block)
    pix_shape = (3, sub_n, 8, block)
    halo_shape = (2, slices, 1, width)
    delta, pixels, base = pl.pallas_call(
        functools.partial(rays_kernel, sub_n, slab_n),
        out_shape=(
            jax.ShapeDtypeStruct(delta_shape, jnp.float32),
            jax.ShapeDtypeStruct(pix_shape, jnp.int32),
            jax.ShapeDtypeStruct((slices, rows, width), jnp.float32),
        ),
        in_specs=[pl.BlockSpec(memory_space=pltpu.HBM)] * 8,
        out_specs=(vmem, vmem, hbm),
        scratch_shapes=[
            pltpu.VMEM(measured.shape, jnp.float32),
            pltpu.SMEM(ray_index.shape, jnp.int32),
            pltpu.SMEM(pixel_index.shape, jnp.int32),
            pltpu.SMEM(step_size.shape, jnp.float32),
            pltpu.SMEM(kernel.shape, jnp.float32),
            pltpu.VMEM((slices, rows + 16, width), jnp.float32),
            pltpu.VMEM((slices, rows, width), jnp.float32),
            pltpu.VMEM((slices, rows, width), jnp.float32),
            pltpu.VMEM((nblk, block, block), jnp.bfloat16),
            pltpu.VMEM((8, block), jnp.int32),
            pltpu.VMEM((inner, slices, ray_blocks, block), jnp.float32),
            pltpu.VMEM((outer, slices, ray_blocks, block), jnp.float32),
            pltpu.VMEM(delta_shape, jnp.float32),
            pltpu.VMEM(pix_shape, jnp.int32),
            pltpu.VMEM(halo_shape, jnp.float32),
            dma((8,)), dma,
            dma((inner,)), dma((inner,)),
            dma((outer,)), dma((outer,)),
            dma((3, sub_n)), dma((3, sub_n)),
            dma((2, 1)), dma((2, 1)),
            dma((3, sub_n)), dma((3, sub_n)),
        ],
        compiler_params=pltpu.CompilerParams(collective_id=0, has_side_effects=True),
        name="rays",
    )(z_field, duals, tiles, measured, ray_index, pixel_index, step_size, kernel)
    return pl.pallas_call(
        field_kernel,
        out_shape=(
            jax.ShapeDtypeStruct((slices, rows, width), jnp.float32),
            jax.ShapeDtypeStruct((1, slices, rows, width), jnp.float32),
        ),
        in_specs=[hbm, hbm, vmem, smem, smem],
        out_specs=(hbm, hbm),
        scratch_shapes=[
            pltpu.VMEM((slices, rows + 16, width + 2 * block), jnp.float32),
            pltpu.VMEM((slices, rows, width), jnp.float32),
            dma((2,)), dma((5,)),
        ],

        name="field",
    )(z_field, base, delta, pixels, kernel)


def solution(mesh):
    placed = (
        P(None, "slab", None),
        P("subset", None, "slab", None),
        P("subset", "slab", None, None),
        P("subset", "slab"),
        P("subset", "slab"),
        P("subset", None, None),
        P("subset"),
        P(),
    )
    return jax.shard_map(
        functools.partial(body, mesh.shape["subset"], mesh.shape["slab"]),
        mesh=mesh,
        in_specs=placed,
        out_specs=(P(None, "slab", None), P("subset", None, "slab", None)),
        check_vma=False,
    )
```

```python
import functools
import math

import jax
import jax.numpy as jnp
from jax import lax
from jax.experimental import pallas as pl
from jax.experimental.pallas import tpu as pltpu
from jax.sharding import PartitionSpec as P


MESH = pl.DeviceIdType.MESH


def split_group(count):
    inner = 1
    while inner < min(count, 16) and count % (inner * 2) == 0:
        inner *= 2
    return inner, count // inner


def rays_kernel(
    sub_n, slab_n,
    z_hbm, dual_hbm, tile_hbm, meas_hbm, ray_hbm, pix_hbm, step_hbm, w_hbm,
    delta_out, pix_out, base_out,
    meas_ref, ray_ref, pix_ref, step_ref, w_ref, z_v, dual_v, base_v, tile_v, pix_v, got_in, got_out, delta_v, halo_v,
    load_sem, base_sem, in_send, in_recv, out_send, out_recv,
    pix_send, pix_recv, halo_send, halo_recv, fin_send, fin_recv,
):
    slices, rows, width = z_hbm.shape
    nblk, block = tile_v.shape[0], tile_v.shape[1]
    ray_blocks = got_in.shape[2]
    col_blocks = width // block
    inner, outer = split_group(slab_n)
    sub = lax.axis_index("subset")
    slab = lax.axis_index("slab")
    lane = slab % inner
    tier = slab // inner
    has_up = slab > 0
    has_down = slab < slab_n - 1

    loads = [
        pltpu.make_async_copy(z_hbm, z_v.at[:, pl.ds(8, rows)], load_sem.at[0]),
        pltpu.make_async_copy(dual_hbm.at[0], dual_v, load_sem.at[1]),
        pltpu.make_async_copy(tile_hbm.at[0], tile_v, load_sem.at[2]),
    ]
    pairs = [
        (meas_hbm, meas_ref), (ray_hbm, ray_ref), (pix_hbm, pix_ref),
        (step_hbm, step_ref), (w_hbm, w_ref),
    ]
    smalls = [
        pltpu.make_async_copy(src, dst, load_sem.at[3 + i]) for i, (src, dst) in enumerate(pairs)
    ]
    for load in smalls + loads:
        load.start()

    halo_v[...] = jnp.zeros_like(halo_v)

    in_peers = [(sub, tier * inner + (lane + k) % inner) for k in range(1, inner)]
    out_peers = [(sub, ((tier + k) % outer) * inner + lane) for k in range(1, outer)]
    sub_peers = [((sub + k) % sub_n, slab) for k in range(1, sub_n)]
    barrier = pltpu.get_barrier_semaphore()
    for peer in in_peers + out_peers + sub_peers:
        pl.semaphore_signal(barrier, inc=1, device_id=peer, device_id_type=MESH)

    @pl.when(has_up)
    def _():
        for k in range(sub_n):
            pl.semaphore_signal(
                barrier, inc=1, device_id=((sub + k) % sub_n, slab - 1), device_id_type=MESH
            )

    @pl.when(has_down)
    def _():
        for k in range(sub_n):
            pl.semaphore_signal(
                barrier, inc=1, device_id=((sub + k) % sub_n, slab + 1), device_id_type=MESH
            )

    for load in smalls:
        load.wait()
    columns = lax.broadcasted_iota(jnp.int32, (8, width), 1)
    weights = [[[w_ref[a, b, c] for c in range(3)] for b in range(3)] for a in range(3)]

    def stencil(low, high):
        for s in range(slices):
            def step(g, carry, s=s):
                base = pl.multiple_of(g * 8, 8)
                sums = [None, None, None]
                for a in range(3):
                    if not 0 <= s + a - 1 < slices:
                        continue
                    window = z_v[s + a - 1, pl.ds(base, 24), :]
                    for b in range(3):
                        moved = window[7 + b : 15 + b]
                        if a == 1 and b == 1:
                            middle = moved
                        for c in range(3):
                            term = weights[a][b][c] * moved
                            sums[c] = term if sums[c] is None else sums[c] + term
                left = jnp.where(columns == 0, 0.0, pltpu.roll(sums[0], 1, 1))
                right = jnp.where(columns == width - 1, 0.0, pltpu.roll(sums[2], width - 1, 1))
                base_v[s, pl.ds(base, 8), :] = middle + (sums[1] + left + right)
                return carry

            lax.fori_loop(low, high, step, 0)

    groups = rows // 8
    second_cut = 1 + max(groups - 2, 0) * 10 // 14
    first_cut = second_cut if outer == 1 else (1 + second_cut) // 2

    lanes = lax.broadcasted_iota(jnp.int32, (8, block), 1)
    mine = jnp.zeros((8, block), jnp.int32)
    for n in range(nblk):
        mine = jnp.where(lanes == n, pix_ref[0, n], mine)
    pix_v[...] = mine

    ray_rows = lax.broadcasted_iota(jnp.int32, (ray_blocks, block), 0)
    hot_rows = lax.broadcasted_iota(jnp.int32, (nblk, ray_blocks), 0)
    hot_cols = lax.broadcasted_iota(jnp.int32, (nblk, ray_blocks), 1)
    hot = jnp.zeros((nblk, ray_blocks), jnp.float32)
    for n in range(nblk):
        here = jnp.where(hot_cols == ray_ref[0, n], 1.0, 0.0)
        hot = jnp.where(hot_rows == n, here, hot)
    hot = hot.astype(jnp.bfloat16)
    row_cols = lax.broadcasted_iota(jnp.int32, (nblk, rows), 1)
    row_rows = lax.broadcasted_iota(jnp.int32, (nblk, rows), 0)
    tile_rows = lax.broadcasted_iota(jnp.int32, (nblk, block), 0)
    row_hot = jnp.zeros((nblk, rows), jnp.float32)
    col_of = jnp.zeros((nblk, block), jnp.int32)
    for n in range(nblk):
        here = jnp.where(row_cols == lax.div(pix_ref[0, n], col_blocks), 1.0, 0.0)
        row_hot = jnp.where(row_rows == n, here, row_hot)
        col_of = jnp.where(tile_rows == n, lax.rem(pix_ref[0, n], col_blocks), col_of)
    row_hot = row_hot.astype(jnp.bfloat16)
    for load in loads:
        load.wait()
    for s in range(slices):
        start = jnp.zeros((nblk, block), jnp.float32)
        for c in range(col_blocks):
            at = pl.ds(c * block, block)
            part = (z_v[s, pl.ds(8, rows), at] - dual_v[s, :, at]).astype(jnp.bfloat16)
            part = jnp.dot(row_hot, part, preferred_element_type=jnp.float32)
            start = jnp.where(col_of == c, part, start)
        start = start.astype(jnp.bfloat16)
        total = jnp.zeros((ray_blocks, block), jnp.float32)
        for n in range(nblk):
            term = lax.dot_general(
                start, tile_v[n], (((1,), (1,)), ((), ())), preferred_element_type=jnp.float32
            )
            total = total + jnp.where(ray_rows == ray_ref[0, n], term[n : n + 1], 0.0)
        got_in[lane, s] = total

    targets = []
    for s in range(slices):
        target = jnp.zeros((ray_blocks, block), jnp.float32)
        for k in range(ray_blocks):
            piece = meas_ref[0, pl.ds(s, 1), pl.ds(k * block, block)]
            target = jnp.where(ray_rows == k, piece, target)
        targets.append(target)

    pl.semaphore_wait(
        barrier,
        len(in_peers + out_peers + sub_peers)
        + sub_n * (has_up.astype(jnp.int32) + has_down.astype(jnp.int32)),
    )

    def spread(src, dst, peers, send, recv):
        return [
            pltpu.make_async_remote_copy(
                src_ref=src, dst_ref=dst, send_sem=send.at[k], recv_sem=recv.at[k],
                device_id=peer, device_id_type=MESH,
            )
            for k, peer in enumerate(peers)
        ]

    ins = spread(got_in.at[lane], got_in.at[lane], in_peers, in_send, in_recv)
    for copy in ins:
        copy.start()

    pix_subs = spread(pix_v, pix_out.at[0, sub], sub_peers, pix_send.at[0], pix_recv.at[0])
    above = [((sub + k) % sub_n, slab - 1) for k in range(sub_n)]
    below = [((sub + k) % sub_n, slab + 1) for k in range(sub_n)]
    pix_up = spread(pix_v, pix_out.at[2, sub], above, pix_send.at[1], pix_recv.at[1])
    pix_down = spread(pix_v, pix_out.at[1, sub], below, pix_send.at[2], pix_recv.at[2])
    halo_up = spread(
        z_hbm.at[:, pl.ds(0, 1)], halo_v.at[1], above[:1], halo_send.at[0], halo_recv.at[0]
    )
    halo_down = spread(
        z_hbm.at[:, pl.ds(rows - 1, 1)], halo_v.at[0], below[:1], halo_send.at[1], halo_recv.at[1]
    )
    keeps = [pltpu.make_async_copy(pix_v, pix_out.at[0, sub], base_sem.at[0])]
    for copy in keeps + pix_subs:
        copy.start()

    @pl.when(has_up)
    def _():
        for copy in pix_up + halo_up:
            copy.start()

    @pl.when(has_down)
    def _():
        for copy in pix_down + halo_down:
            copy.start()

    stencil(1, first_cut)
    for copy in ins:
        copy.wait_recv()
    group = got_in[0]
    for k in range(1, inner):
        group = group + got_in[k]
    got_out[tier] = group
    outs = spread(got_out.at[tier], got_out.at[tier], out_peers, out_send, out_recv)
    for copy in outs:
        copy.start()
    stencil(first_cut, second_cut)
    for copy in outs:
        copy.wait_recv()
    full = got_out[0]
    for k in range(1, outer):
        full = full + got_out[k]
    scale = step_ref[0] * (width / math.sqrt(ray_blocks * block))
    for s in range(slices):
        residual = (full[s] - targets[s]).astype(jnp.bfloat16)
        picked = jnp.dot(hot, residual, preferred_element_type=jnp.float32).astype(jnp.bfloat16)
        delta = jnp.zeros((nblk, block), jnp.float32)
        for n in range(nblk):
            term = jnp.dot(picked, tile_v[n], preferred_element_type=jnp.float32)
            delta = jnp.where(tile_rows == n, term, delta)
        delta = delta * scale
        delta_v[s] = delta

    fin_subs = spread(delta_v, delta_out.at[0, sub], sub_peers, fin_send.at[0], fin_recv.at[0])
    fin_up = spread(delta_v, delta_out.at[2, sub], above, fin_send.at[1], fin_recv.at[1])
    fin_down = spread(delta_v, delta_out.at[1, sub], below, fin_send.at[2], fin_recv.at[2])

    @pl.when(has_up)
    def _():
        for copy in fin_up:
            copy.start()

    @pl.when(has_down)
    def _():
        for copy in fin_down:
            copy.start()

    keeps.append(pltpu.make_async_copy(delta_v, delta_out.at[0, sub], base_sem.at[1]))
    for copy in fin_subs + keeps[1:]:
        copy.start()
    stencil(second_cut, max(groups - 1, 1))

    @pl.when(has_down)
    def _():
        for copy in halo_up:
            copy.wait_recv()

    @pl.when(has_up)
    def _():
        for copy in halo_down:
            copy.wait_recv()

    z_v[:, pl.ds(7, 1), :] = halo_v[0]
    z_v[:, pl.ds(8 + rows, 1), :] = halo_v[1]
    stencil(0, 1)
    if groups > 1:
        stencil(groups - 1, groups)
    keeps.append(pltpu.make_async_copy(base_v, base_out, base_sem.at[2]))
    keeps[2].start()
    for copy in ins + outs:
        copy.wait_send()
    for copy in pix_subs + fin_subs:
        copy.wait()

    @pl.when(has_up)
    def _():
        for copy in pix_up + halo_up + fin_up:
            copy.wait_send()
        for copy in pix_down + fin_down:
            copy.wait_recv()

    @pl.when(has_down)
    def _():
        for copy in pix_down + halo_down + fin_down:
            copy.wait_send()
        for copy in pix_up + fin_up:
            copy.wait_recv()

    for copy in keeps:
        copy.wait()


def field_kernel(
    slab_n, z_hbm, base_hbm, delta_hbm, pix_hbm, w_hbm,
    field_hbm, dual_hbm,
    delta_ref, pix_ref, w_ref, field_v, own_v, load_sem, store_sem,
):
    slices, rows, width = own_v.shape
    sub_n, nblk, block = delta_ref.shape[1], delta_ref.shape[3], delta_ref.shape[4]
    col_blocks = width // block
    sub = lax.axis_index("subset")
    slab = lax.axis_index("slab")
    inside = (slice(None), pl.ds(8, rows), pl.ds(block, width))
    loads = [
        pltpu.make_async_copy(base_hbm, field_v.at[inside], load_sem.at[0]),
        pltpu.make_async_copy(z_hbm, own_v, load_sem.at[1]),
    ]
    smalls = [
        pltpu.make_async_copy(delta_hbm, delta_ref, load_sem.at[2]),
        pltpu.make_async_copy(pix_hbm, pix_ref, load_sem.at[3]),
        pltpu.make_async_copy(w_hbm, w_ref, load_sem.at[4]),
    ]
    for load in smalls + loads:
        load.start()
    for load in smalls:
        load.wait()
    weights = [[[w_ref[a, b, c] for c in range(3)] for b in range(3)] for a in range(3)]
    share = -1.0 / sub_n
    sublanes = lax.broadcasted_iota(jnp.int32, (8, block), 0)
    window_rows = lax.broadcasted_iota(jnp.int32, (16, 3 * block), 0)
    zeros = jnp.zeros((1, block), jnp.float32)

    def patch(place, i, n, row, col):
        base = pl.multiple_of((row - 1) // 8 * 8, 8)
        step = window_rows - (row - 1 - base)
        for s in range(slices):
            delta = delta_ref[place, i, s, pl.ds(n, 1), :] * share
            wide = jnp.concatenate([zeros, delta, zeros], axis=1)
            left = pltpu.roll(wide, 1, 1)
            right = pltpu.roll(wide, 3 * block - 1, 1)
            for a in range(3):
                out = s + 1 - a
                if not 0 <= out < slices:
                    continue
                sums = [w[0] * left + w[1] * wide + w[2] * right for w in weights[a]]
                if a == 1:
                    sums[1] = sums[1] + wide
                add = jnp.where(step == 2, sums[0], 0.0)
                add = jnp.where(step == 1, sums[1], add)
                add = jnp.where(step == 0, sums[2], add)
                at = (out, pl.ds(base, 16), pl.ds(col, 3 * block))
                field_v[at] = field_v[at] + add

    for load in loads:
        load.wait()
    for place in range(3):
        for i in range(sub_n):
            for n in range(nblk):
                pixel = pix_ref[place, i, 0, n]
                row = pixel // col_blocks
                col = pl.multiple_of((pixel % col_blocks) * block, block)
                if place == 0:
                    patch(place, i, n, row + 8, col)
                elif place == 1:
                    pl.when((slab > 0) & (row == rows - 1))(functools.partial(patch, place, i, n, 7, col))
                else:
                    pl.when((slab < slab_n - 1) & (row == 0))(functools.partial(patch, place, i, n, rows + 8, col))
    stores = [pltpu.make_async_copy(field_v.at[inside], field_hbm, store_sem.at[0])]
    stores[0].start()
    for n in range(nblk):
        pixel = pix_ref[0, sub, 0, n]
        row = pixel // col_blocks
        col = pl.multiple_of((pixel % col_blocks) * block, block)
        base = pl.multiple_of(row // 8 * 8, 8)
        for s in range(slices):
            at = (s, pl.ds(base, 8), pl.ds(col, block))
            value = delta_ref[0, sub, s, pl.ds(n, 1), :]
            own_v[at] = own_v[at] - jnp.where(sublanes == row % 8, value, 0.0)
    parts = 4 if rows % 32 == 0 else 1
    size = rows // parts
    for part in range(parts):
        for s in range(slices):
            def step(g, carry, s=s, part=part):
                at = pl.multiple_of(part * size + g * 8, 8)
                field = field_v[s, pl.ds(at + 8, 8), pl.ds(block, width)]
                own_v[s, pl.ds(at, 8), :] = own_v[s, pl.ds(at, 8), :] - field
                return carry

            lax.fori_loop(0, size // 8, step, 0)
        span = (slice(None), pl.ds(part * size, size))
        stores.append(
            pltpu.make_async_copy(own_v.at[span], dual_hbm.at[(0, *span)], store_sem.at[1 + part])
        )
        stores[-1].start()
    for store in stores:
        store.wait()


def body(sub_n, slab_n, z_field, duals, tiles, ray_index, pixel_index, measured, step_size, kernel):
    slices, rows, width = z_field.shape
    nblk, block = tiles.shape[1], tiles.shape[2]
    ray_blocks = measured.shape[2] // block
    inner, outer = split_group(slab_n)
    hbm = pl.BlockSpec(memory_space=pl.ANY)
    dma = pltpu.SemaphoreType.DMA
    delta_shape = (3, sub_n, slices, nblk, block)
    pix_shape = (3, sub_n, 8, block)
    halo_shape = (2, slices, 1, width)
    delta, pixels, base = pl.pallas_call(
        functools.partial(rays_kernel, sub_n, slab_n),
        out_shape=(
            jax.ShapeDtypeStruct(delta_shape, jnp.float32),
            jax.ShapeDtypeStruct(pix_shape, jnp.int32),
            jax.ShapeDtypeStruct((slices, rows, width), jnp.float32),
        ),
        in_specs=[hbm] * 8,
        out_specs=(hbm, hbm, hbm),
        scratch_shapes=[
            pltpu.VMEM(measured.shape, jnp.float32),
            pltpu.SMEM(ray_index.shape, jnp.int32),
            pltpu.SMEM(pixel_index.shape, jnp.int32),
            pltpu.SMEM(step_size.shape, jnp.float32),
            pltpu.SMEM(kernel.shape, jnp.float32),
            pltpu.VMEM((slices, rows + 16, width), jnp.float32),
            pltpu.VMEM((slices, rows, width), jnp.float32),
            pltpu.VMEM((slices, rows, width), jnp.float32),
            pltpu.VMEM((nblk, block, block), jnp.bfloat16),
            pltpu.VMEM((8, block), jnp.int32),
            pltpu.VMEM((inner, slices, ray_blocks, block), jnp.float32),
            pltpu.VMEM((outer, slices, ray_blocks, block), jnp.float32),
            pltpu.VMEM((slices, nblk, block), jnp.float32),
            pltpu.VMEM(halo_shape, jnp.float32),
            dma((8,)), dma((3,)),
            dma((inner,)), dma((inner,)),
            dma((outer,)), dma((outer,)),
            dma((3, sub_n)), dma((3, sub_n)),
            dma((2, 1)), dma((2, 1)),
            dma((3, sub_n)), dma((3, sub_n)),
        ],
        compiler_params=pltpu.CompilerParams(collective_id=0, has_side_effects=True),
        name="rays",
    )(z_field, duals, tiles, measured, ray_index, pixel_index, step_size, kernel)
    return pl.pallas_call(
        functools.partial(field_kernel, slab_n),
        out_shape=(
            jax.ShapeDtypeStruct((slices, rows, width), jnp.float32),
            jax.ShapeDtypeStruct((1, slices, rows, width), jnp.float32),
        ),
        in_specs=[hbm] * 5,
        out_specs=(hbm, hbm),
        scratch_shapes=[
            pltpu.VMEM(delta_shape, jnp.float32),
            pltpu.SMEM(pix_shape, jnp.int32),
            pltpu.SMEM(kernel.shape, jnp.float32),
            pltpu.VMEM((slices, rows + 16, width + 2 * block), jnp.float32),
            pltpu.VMEM((slices, rows, width), jnp.float32),
            dma((5,)), dma((5,)),
        ],

        name="field",
    )(z_field, base, delta, pixels, kernel)


def solution(mesh):
    placed = (
        P(None, "slab", None),
        P("subset", None, "slab", None),
        P("subset", "slab", None, None),
        P("subset", "slab"),
        P("subset", "slab"),
        P("subset", None, None),
        P("subset"),
        P(),
    )
    return jax.shard_map(
        functools.partial(body, mesh.shape["subset"], mesh.shape["slab"]),
        mesh=mesh,
        in_specs=placed,
        out_specs=(P(None, "slab", None), P("subset", None, "slab", None)),
        check_vma=False,
    )
```

```python
import functools
import math

import jax
import jax.numpy as jnp
from jax import lax
from jax.experimental import pallas as pl
from jax.experimental.pallas import tpu as pltpu
from jax.sharding import PartitionSpec as P

GRANT = 16 * 1024 * 1024
MESH = pl.DeviceIdType.MESH


def split_group(count):
    inner = 1
    while inner < min(count, 16) and count % (inner * 2) == 0:
        inner *= 2
    return inner, count // inner


def rays_kernel(
    sub_n, slab_n,
    z_hbm, dual_hbm, tile_hbm, meas_hbm, ray_hbm, pix_hbm, step_hbm, w_hbm,
    delta_out, pix_out, base_out,
    meas_ref, ray_ref, pix_ref, step_ref, w_ref, z_v, dual_v, base_v, tile_v, pix_v, got_in, got_out, delta_v, halo_v,
    load_sem, base_sem, in_send, in_recv, out_send, out_recv,
    pix_send, pix_recv, halo_send, halo_recv, fin_send, fin_recv,
):
    slices, rows, width = z_hbm.shape
    nblk, block = tile_v.shape[0], tile_v.shape[1]
    ray_blocks = got_in.shape[2]
    col_blocks = width // block
    inner, outer = split_group(slab_n)
    sub = lax.axis_index("subset")
    slab = lax.axis_index("slab")
    lane = slab % inner
    tier = slab // inner
    has_up = slab > 0
    has_down = slab < slab_n - 1

    loads = [
        pltpu.make_async_copy(z_hbm, z_v.at[:, pl.ds(8, rows)], load_sem.at[0]),
        pltpu.make_async_copy(dual_hbm.at[0], dual_v, load_sem.at[1]),
        pltpu.make_async_copy(tile_hbm.at[0], tile_v, load_sem.at[2]),
    ]
    pairs = [
        (meas_hbm, meas_ref), (ray_hbm, ray_ref), (pix_hbm, pix_ref),
        (step_hbm, step_ref), (w_hbm, w_ref),
    ]
    smalls = [
        pltpu.make_async_copy(src, dst, load_sem.at[3 + i]) for i, (src, dst) in enumerate(pairs)
    ]
    for load in smalls + loads:
        load.start()

    halo_v[...] = jnp.zeros_like(halo_v)

    in_peers = [(sub, tier * inner + (lane + k) % inner) for k in range(1, inner)]
    out_peers = [(sub, ((tier + k) % outer) * inner + lane) for k in range(1, outer)]
    sub_peers = [((sub + k) % sub_n, slab) for k in range(1, sub_n)]
    barrier = pltpu.get_barrier_semaphore()
    for peer in in_peers + out_peers + sub_peers:
        pl.semaphore_signal(barrier, inc=1, device_id=peer, device_id_type=MESH)

    @pl.when(has_up)
    def _():
        for k in range(sub_n):
            pl.semaphore_signal(
                barrier, inc=1, device_id=((sub + k) % sub_n, slab - 1), device_id_type=MESH
            )

    @pl.when(has_down)
    def _():
        for k in range(sub_n):
            pl.semaphore_signal(
                barrier, inc=1, device_id=((sub + k) % sub_n, slab + 1), device_id_type=MESH
            )

    for load in smalls:
        load.wait()
    columns = lax.broadcasted_iota(jnp.int32, (8, width), 1)
    weights = [[[w_ref[a, b, c] for c in range(3)] for b in range(3)] for a in range(3)]

    def stencil(low, high):
        for s in range(slices):
            def step(g, carry, s=s):
                base = pl.multiple_of(g * 8, 8)
                sums = [None, None, None]
                for a in range(3):
                    if not 0 <= s + a - 1 < slices:
                        continue
                    window = z_v[s + a - 1, pl.ds(base, 24), :]
                    for b in range(3):
                        moved = window[7 + b : 15 + b]
                        if a == 1 and b == 1:
                            middle = moved
                        for c in range(3):
                            term = weights[a][b][c] * moved
                            sums[c] = term if sums[c] is None else sums[c] + term
                left = jnp.where(columns == 0, 0.0, pltpu.roll(sums[0], 1, 1))
                right = jnp.where(columns == width - 1, 0.0, pltpu.roll(sums[2], width - 1, 1))
                base_v[s, pl.ds(base, 8), :] = middle + (sums[1] + left + right)
                return carry

            lax.fori_loop(low, high, step, 0)

    groups = rows // 8
    second_cut = 1 + max(groups - 2, 0) * 10 // 14
    first_cut = second_cut if outer == 1 else (1 + second_cut) // 2

    lanes = lax.broadcasted_iota(jnp.int32, (8, block), 1)
    mine = jnp.zeros((8, block), jnp.int32)
    for n in range(nblk):
        mine = jnp.where(lanes == n, pix_ref[0, n], mine)
    pix_v[...] = mine

    ray_rows = lax.broadcasted_iota(jnp.int32, (ray_blocks, block), 0)
    hot_rows = lax.broadcasted_iota(jnp.int32, (nblk, ray_blocks), 0)
    hot_cols = lax.broadcasted_iota(jnp.int32, (nblk, ray_blocks), 1)
    hot = jnp.zeros((nblk, ray_blocks), jnp.float32)
    for n in range(nblk):
        here = jnp.where(hot_cols == ray_ref[0, n], 1.0, 0.0)
        hot = jnp.where(hot_rows == n, here, hot)
    hot = hot.astype(jnp.bfloat16)
    row_cols = lax.broadcasted_iota(jnp.int32, (nblk, rows), 1)
    row_rows = lax.broadcasted_iota(jnp.int32, (nblk, rows), 0)
    tile_rows = lax.broadcasted_iota(jnp.int32, (nblk, block), 0)
    row_hot = jnp.zeros((nblk, rows), jnp.float32)
    col_of = jnp.zeros((nblk, block), jnp.int32)
    for n in range(nblk):
        here = jnp.where(row_cols == lax.div(pix_ref[0, n], col_blocks), 1.0, 0.0)
        row_hot = jnp.where(row_rows == n, here, row_hot)
        col_of = jnp.where(tile_rows == n, lax.rem(pix_ref[0, n], col_blocks), col_of)
    row_hot = row_hot.astype(jnp.bfloat16)
    for load in loads:
        load.wait()
    for s in range(slices):
        start = jnp.zeros((nblk, block), jnp.float32)
        for c in range(col_blocks):
            at = pl.ds(c * block, block)
            part = (z_v[s, pl.ds(8, rows), at] - dual_v[s, :, at]).astype(jnp.bfloat16)
            part = jnp.dot(row_hot, part, preferred_element_type=jnp.float32)
            start = jnp.where(col_of == c, part, start)
        start = start.astype(jnp.bfloat16)
        total = jnp.zeros((ray_blocks, block), jnp.float32)
        for n in range(nblk):
            term = lax.dot_general(
                start, tile_v[n], (((1,), (1,)), ((), ())), preferred_element_type=jnp.float32
            )
            total = total + jnp.where(ray_rows == ray_ref[0, n], term[n : n + 1], 0.0)
        got_in[lane, s] = total

    targets = []
    for s in range(slices):
        target = jnp.zeros((ray_blocks, block), jnp.float32)
        for k in range(ray_blocks):
            piece = meas_ref[0, pl.ds(s, 1), pl.ds(k * block, block)]
            target = jnp.where(ray_rows == k, piece, target)
        targets.append(target)

    pl.semaphore_wait(
        barrier,
        len(in_peers + out_peers + sub_peers)
        + sub_n * (has_up.astype(jnp.int32) + has_down.astype(jnp.int32)),
    )

    def spread(src, dst, peers, send, recv):
        return [
            pltpu.make_async_remote_copy(
                src_ref=src, dst_ref=dst, send_sem=send.at[k], recv_sem=recv.at[k],
                device_id=peer, device_id_type=MESH,
            )
            for k, peer in enumerate(peers)
        ]

    ins = spread(got_in.at[lane], got_in.at[lane], in_peers, in_send, in_recv)
    for copy in ins:
        copy.start()

    pix_subs = spread(pix_v, pix_out.at[0, sub], sub_peers, pix_send.at[0], pix_recv.at[0])
    above = [((sub + k) % sub_n, slab - 1) for k in range(sub_n)]
    below = [((sub + k) % sub_n, slab + 1) for k in range(sub_n)]
    pix_up = spread(pix_v, pix_out.at[2, sub], above, pix_send.at[1], pix_recv.at[1])
    pix_down = spread(pix_v, pix_out.at[1, sub], below, pix_send.at[2], pix_recv.at[2])
    halo_up = spread(
        z_hbm.at[:, pl.ds(0, 1)], halo_v.at[1], above[:1], halo_send.at[0], halo_recv.at[0]
    )
    halo_down = spread(
        z_hbm.at[:, pl.ds(rows - 1, 1)], halo_v.at[0], below[:1], halo_send.at[1], halo_recv.at[1]
    )
    keeps = [pltpu.make_async_copy(pix_v, pix_out.at[0, sub], base_sem.at[0])]
    for copy in keeps + pix_subs:
        copy.start()

    @pl.when(has_up)
    def _():
        for copy in pix_up + halo_up:
            copy.start()

    @pl.when(has_down)
    def _():
        for copy in pix_down + halo_down:
            copy.start()

    stencil(1, first_cut)
    for copy in ins:
        copy.wait_recv()
    group = got_in[0]
    for k in range(1, inner):
        group = group + got_in[k]
    got_out[tier] = group
    outs = spread(got_out.at[tier], got_out.at[tier], out_peers, out_send, out_recv)
    for copy in outs:
        copy.start()
    stencil(first_cut, second_cut)
    for copy in outs:
        copy.wait_recv()
    full = got_out[0]
    for k in range(1, outer):
        full = full + got_out[k]
    scale = step_ref[0] * (width / math.sqrt(ray_blocks * block))
    for s in range(slices):
        residual = (full[s] - targets[s]).astype(jnp.bfloat16)
        picked = jnp.dot(hot, residual, preferred_element_type=jnp.float32).astype(jnp.bfloat16)
        delta = jnp.zeros((nblk, block), jnp.float32)
        for n in range(nblk):
            term = jnp.dot(picked, tile_v[n], preferred_element_type=jnp.float32)
            delta = jnp.where(tile_rows == n, term, delta)
        delta = delta * scale
        delta_v[s] = delta

    fin_subs = spread(delta_v, delta_out.at[0, sub], sub_peers, fin_send.at[0], fin_recv.at[0])
    fin_up = spread(delta_v, delta_out.at[2, sub], above, fin_send.at[1], fin_recv.at[1])
    fin_down = spread(delta_v, delta_out.at[1, sub], below, fin_send.at[2], fin_recv.at[2])

    @pl.when(has_up)
    def _():
        for copy in fin_up:
            copy.start()

    @pl.when(has_down)
    def _():
        for copy in fin_down:
            copy.start()

    keeps.append(pltpu.make_async_copy(delta_v, delta_out.at[0, sub], base_sem.at[1]))
    for copy in fin_subs + keeps[1:]:
        copy.start()
    stencil(second_cut, max(groups - 1, 1))

    @pl.when(has_down)
    def _():
        for copy in halo_up:
            copy.wait_recv()

    @pl.when(has_up)
    def _():
        for copy in halo_down:
            copy.wait_recv()

    z_v[:, pl.ds(7, 1), :] = halo_v[0]
    z_v[:, pl.ds(8 + rows, 1), :] = halo_v[1]
    stencil(0, 1)
    if groups > 1:
        stencil(groups - 1, groups)
    keeps.append(pltpu.make_async_copy(base_v, base_out, base_sem.at[2]))
    keeps[2].start()
    for copy in ins + outs:
        copy.wait_send()
    for copy in pix_subs + fin_subs:
        copy.wait()

    @pl.when(has_up)
    def _():
        for copy in pix_up + halo_up + fin_up:
            copy.wait_send()
        for copy in pix_down + fin_down:
            copy.wait_recv()

    @pl.when(has_down)
    def _():
        for copy in pix_down + halo_down + fin_down:
            copy.wait_send()
        for copy in pix_up + fin_up:
            copy.wait_recv()

    for copy in keeps:
        copy.wait()


def field_kernel(
    slab_n, z_hbm, base_hbm, delta_hbm, pix_hbm, w_hbm,
    field_hbm, dual_hbm,
    delta_ref, pix_ref, w_ref, field_v, own_v, load_sem, store_sem,
):
    slices, rows, width = own_v.shape
    sub_n, nblk, block = delta_ref.shape[1], delta_ref.shape[3], delta_ref.shape[4]
    col_blocks = width // block
    sub = lax.axis_index("subset")
    slab = lax.axis_index("slab")
    inside = (slice(None), pl.ds(8, rows), pl.ds(block, width))
    loads = [
        pltpu.make_async_copy(base_hbm, field_v.at[inside], load_sem.at[0]),
        pltpu.make_async_copy(z_hbm, own_v, load_sem.at[1]),
    ]
    smalls = [
        pltpu.make_async_copy(delta_hbm, delta_ref, load_sem.at[2]),
        pltpu.make_async_copy(pix_hbm, pix_ref, load_sem.at[3]),
        pltpu.make_async_copy(w_hbm, w_ref, load_sem.at[4]),
    ]
    for load in smalls + loads:
        load.start()
    for load in smalls:
        load.wait()
    weights = [[[w_ref[a, b, c] for c in range(3)] for b in range(3)] for a in range(3)]
    share = -1.0 / sub_n
    sublanes = lax.broadcasted_iota(jnp.int32, (8, block), 0)
    window_rows = lax.broadcasted_iota(jnp.int32, (16, 3 * block), 0)
    zeros = jnp.zeros((1, block), jnp.float32)

    def patch(place, i, n, row, col):
        base = pl.multiple_of((row - 1) // 8 * 8, 8)
        step = window_rows - (row - 1 - base)
        for s in range(slices):
            delta = delta_ref[place, i, s, pl.ds(n, 1), :] * share
            wide = jnp.concatenate([zeros, delta, zeros], axis=1)
            left = pltpu.roll(wide, 1, 1)
            right = pltpu.roll(wide, 3 * block - 1, 1)
            for a in range(3):
                out = s + 1 - a
                if not 0 <= out < slices:
                    continue
                sums = [w[0] * left + w[1] * wide + w[2] * right for w in weights[a]]
                if a == 1:
                    sums[1] = sums[1] + wide
                add = jnp.where(step == 2, sums[0], 0.0)
                add = jnp.where(step == 1, sums[1], add)
                add = jnp.where(step == 0, sums[2], add)
                at = (out, pl.ds(base, 16), pl.ds(col, 3 * block))
                field_v[at] = field_v[at] + add

    for load in loads:
        load.wait()
    for place in range(3):
        for i in range(sub_n):
            for n in range(nblk):
                pixel = pix_ref[place, i, 0, n]
                row = pixel // col_blocks
                col = pl.multiple_of((pixel % col_blocks) * block, block)
                if place == 0:
                    patch(place, i, n, row + 8, col)
                elif place == 1:
                    pl.when((slab > 0) & (row == rows - 1))(functools.partial(patch, place, i, n, 7, col))
                else:
                    pl.when((slab < slab_n - 1) & (row == 0))(functools.partial(patch, place, i, n, rows + 8, col))
    stores = [pltpu.make_async_copy(field_v.at[inside], field_hbm, store_sem.at[0])]
    stores[0].start()
    for n in range(nblk):
        pixel = pix_ref[0, sub, 0, n]
        row = pixel // col_blocks
        col = pl.multiple_of((pixel % col_blocks) * block, block)
        base = pl.multiple_of(row // 8 * 8, 8)
        for s in range(slices):
            at = (s, pl.ds(base, 8), pl.ds(col, block))
            value = delta_ref[0, sub, s, pl.ds(n, 1), :]
            own_v[at] = own_v[at] - jnp.where(sublanes == row % 8, value, 0.0)
    parts = 4 if rows % 32 == 0 else 1
    size = rows // parts
    for part in range(parts):
        for s in range(slices):
            def step(g, carry, s=s, part=part):
                at = pl.multiple_of(part * size + g * 8, 8)
                field = field_v[s, pl.ds(at + 8, 8), pl.ds(block, width)]
                own_v[s, pl.ds(at, 8), :] = own_v[s, pl.ds(at, 8), :] - field
                return carry

            lax.fori_loop(0, size // 8, step, 0)
        span = (slice(None), pl.ds(part * size, size))
        stores.append(
            pltpu.make_async_copy(own_v.at[span], dual_hbm.at[(0, *span)], store_sem.at[1 + part])
        )
        stores[-1].start()
    for store in stores:
        store.wait()


def body(sub_n, slab_n, z_field, duals, tiles, ray_index, pixel_index, measured, step_size, kernel):
    slices, rows, width = z_field.shape
    nblk, block = tiles.shape[1], tiles.shape[2]
    ray_blocks = measured.shape[2] // block
    inner, outer = split_group(slab_n)
    hbm = pl.BlockSpec(memory_space=pl.ANY)
    dma = pltpu.SemaphoreType.DMA
    delta_shape = (3, sub_n, slices, nblk, block)
    pix_shape = (3, sub_n, 8, block)
    halo_shape = (2, slices, 1, width)
    pinned = [
        pltpu.with_memory_space_constraint(x, pltpu.HBM)
        for x in (z_field, duals, tiles, measured, ray_index, pixel_index, kernel)
    ]
    delta, pixels, base = pl.pallas_call(
        functools.partial(rays_kernel, sub_n, slab_n),
        out_shape=(
            jax.ShapeDtypeStruct(delta_shape, jnp.float32),
            jax.ShapeDtypeStruct(pix_shape, jnp.int32),
            jax.ShapeDtypeStruct((slices, rows, width), jnp.float32),
        ),
        in_specs=[pl.BlockSpec(memory_space=pltpu.HBM)] * 6 + [hbm, pl.BlockSpec(memory_space=pltpu.HBM)],
        out_specs=(hbm, hbm, hbm),
        scratch_shapes=[
            pltpu.VMEM(measured.shape, jnp.float32),
            pltpu.SMEM(ray_index.shape, jnp.int32),
            pltpu.SMEM(pixel_index.shape, jnp.int32),
            pltpu.SMEM(step_size.shape, jnp.float32),
            pltpu.SMEM(kernel.shape, jnp.float32),
            pltpu.VMEM((slices, rows + 16, width), jnp.float32),
            pltpu.VMEM((slices, rows, width), jnp.float32),
            pltpu.VMEM((slices, rows, width), jnp.float32),
            pltpu.VMEM((nblk, block, block), jnp.bfloat16),
            pltpu.VMEM((8, block), jnp.int32),
            pltpu.VMEM((inner, slices, ray_blocks, block), jnp.float32),
            pltpu.VMEM((outer, slices, ray_blocks, block), jnp.float32),
            pltpu.VMEM((slices, nblk, block), jnp.float32),
            pltpu.VMEM(halo_shape, jnp.float32),
            dma((8,)), dma((3,)),
            dma((inner,)), dma((inner,)),
            dma((outer,)), dma((outer,)),
            dma((3, sub_n)), dma((3, sub_n)),
            dma((2, 1)), dma((2, 1)),
            dma((3, sub_n)), dma((3, sub_n)),
        ],
        compiler_params=pltpu.CompilerParams(collective_id=0, has_side_effects=True, vmem_limit_bytes=GRANT),
        name="rays",
    )(*pinned[:6], step_size, pinned[6])
    return pl.pallas_call(
        functools.partial(field_kernel, slab_n),
        out_shape=(
            jax.ShapeDtypeStruct((slices, rows, width), jnp.float32),
            jax.ShapeDtypeStruct((1, slices, rows, width), jnp.float32),
        ),
        in_specs=[hbm] * 5,
        out_specs=(hbm, hbm),
        scratch_shapes=[
            pltpu.VMEM(delta_shape, jnp.float32),
            pltpu.SMEM(pix_shape, jnp.int32),
            pltpu.SMEM(kernel.shape, jnp.float32),
            pltpu.VMEM((slices, rows + 16, width + 2 * block), jnp.float32),
            pltpu.VMEM((slices, rows, width), jnp.float32),
            dma((5,)), dma((5,)),
        ],

        compiler_params=pltpu.CompilerParams(vmem_limit_bytes=GRANT),
        name="field",
    )(z_field, base, delta, pixels, kernel)


def solution(mesh):
    placed = (
        P(None, "slab", None),
        P("subset", None, "slab", None),
        P("subset", "slab", None, None),
        P("subset", "slab"),
        P("subset", "slab"),
        P("subset", None, None),
        P("subset"),
        P(),
    )
    return jax.shard_map(
        functools.partial(body, mesh.shape["subset"], mesh.shape["slab"]),
        mesh=mesh,
        in_specs=placed,
        out_specs=(P(None, "slab", None), P("subset", None, "slab", None)),
        check_vma=False,
    )
```
